32 devices in a mesh: clus: 8 (over z, x), ang: 4 (over y, core).
Axes of the slice: x: 2, y: 2, z: 4, core: 2. Of those that a mesh axis runs over, the one named last changes fastest.
Arguments:
- residual: bfloat16 [64, 2, 32, 128], P('clus', None, 'ang'), may hold values from -6 to 6
- margin_ids: int32 [64, 7], replicated, may hold values from 0 to 63, as said below
- block_row: int32 [64, 9], P('clus'), may hold values from 0 to 7, as said below
- block_col: int32 [64, 9], P('clus'), may hold values from 0 to 7, as said below
- inv_blocks: bfloat16 [64, 9, 2, 128, 128], P('clus'), may hold values from -0.375 to 0.375
Outputs:
- preconditioned: float32 [64, 2, 32, 128], P('clus', None, 'ang')
The draws below stay inside these ranges and needn't reach their ends.
Inputs may be any that keep to these rules, and one draw needn't show every extreme that they name: `margin_ids`: cluster c lies on device c // 8 of clus. The margin clusters of the 8 subdomains of one device all lie on other devices; at most 8 of that device's entries name clusters of any one other device, and some device receives exactly 8 of them. `block_row`: each subdomain's blocks write every one of its 8 slots. `block_col`: each subdomain's blocks read every one of its 8 slots.
All inputs are finite; a program needn't handle non-finite values.
Results may differ from the reference program's by a relative error of at most 0.0029.
Values may be sent and summed in bfloat16 or wider, within the bound.
A program may use at most 64 MiB of HBM per device.

```python
import jax
import jax.numpy as jnp
from jax import lax

P_SIZE = 128
K = 8
BLK = 9
ANGLES = 32
CL_DEV = 8
NCLUS = 64
CAP = 8


def draw_margin_ids(key, part):
    device_count = NCLUS // CL_DEV
    request_count = CL_DEV * (K - 1)
    slot_total = (device_count - 1) * CAP
    offsets = 1 + jnp.arange(slot_total, dtype=jnp.int32) // CAP

    def per_device(device):
        device_key = jax.random.fold_in(key, device)
        key_favored, key_jitter, key_place, key_local = jax.random.split(device_key, 4)
        favored = jax.random.randint(key_favored, (), 1, device_count)
        jitter = jax.random.randint(key_jitter, (slot_total,), 0, 1 << 20)
        counter = jnp.arange(slot_total, dtype=jnp.int32)
        scores = jitter * slot_total + counter
        scores = jnp.where(offsets == favored, counter - slot_total, scores)
        ranking = jnp.argsort(scores, stable=True)
        picked = offsets[ranking[:request_count]]
        picked = picked[jax.random.permutation(key_place, request_count)]
        targets = (device + picked) % device_count
        within = jax.random.randint(key_local, (request_count,), 0, CL_DEV)
        return (targets * CL_DEV + within).astype(jnp.int32).reshape(CL_DEV, K - 1)
    tables = jax.vmap(per_device)(jnp.arange(device_count, dtype=jnp.int32))
    return tables.reshape(NCLUS, K - 1).astype(jnp.int32)


def block_pattern(key):
    extra_count = BLK - K

    def per_subdomain(index):
        sub_key = jax.random.fold_in(jax.random.fold_in(key, 11), index)
        key_first, key_rows, key_cols, key_order = jax.random.split(sub_key, 4)
        first_rows = jax.random.permutation(key_first, K).astype(jnp.int32)
        more_rows = jax.random.randint(key_rows, (extra_count,), 0, K).astype(jnp.int32)
        first_cols = jnp.arange(K, dtype=jnp.int32)
        more_cols = jax.random.randint(key_cols, (extra_count,), 0, K).astype(jnp.int32)
        rows_all = jnp.concatenate([first_rows, more_rows])
        cols_all = jnp.concatenate([first_cols, more_cols])
        shuffle = jax.random.permutation(key_order, BLK)
        return (rows_all[shuffle], cols_all[shuffle])
    return jax.vmap(per_subdomain)(jnp.arange(NCLUS, dtype=jnp.int32))


def draw_block_row(key, part):
    return block_pattern(key)[0].astype(jnp.int32)


def draw_block_col(key, part):
    return block_pattern(key)[1].astype(jnp.int32)


def block_levels(key, extent, shards, least, top_value):
    factor_of = 1.0
    for dim, blocks in shards:
        draws = jax.random.uniform(jax.random.fold_in(jax.random.fold_in(key, 6), dim), (blocks,), jnp.float32, least / len(shards), top_value / len(shards))
        factor_of = factor_of * jnp.repeat(jnp.exp(draws), extent[dim] // blocks).reshape((-1,) + (1,) * (len(extent) - 1 - dim))
    return factor_of


def normal_values(own_key, dims, scale, bound, pieces=(), kind=jnp.bfloat16):
    values = jax.random.normal(own_key, dims, jnp.float32) * scale
    if len(pieces) > 0:
        values = block_levels(own_key, dims, pieces, -0.22, 0.18) * values
    return jnp.clip(values, min=-bound, max=bound).astype(kind)


def setup_inputs(seed: int = 0) -> dict:
    seeds = jax.random.split(jax.random.key(seed), 6)
    return {
        "residual": normal_values(seeds[0], (NCLUS, 2, ANGLES, P_SIZE), 1.0, 6.0, ((0, 8), (2, 4))),
        "margin_ids": draw_margin_ids(jax.random.fold_in(seeds[5], 71), 0),
        "block_row": draw_block_row(jax.random.fold_in(seeds[5], 71), 0),
        "block_col": draw_block_col(jax.random.fold_in(seeds[5], 71), 0),
        "inv_blocks": normal_values(seeds[4], (NCLUS, BLK, 2, P_SIZE, P_SIZE), (2 * P_SIZE) ** -0.5, 0.375, ((0, 8),)),
    }


def reference(residual, margin_ids, block_row, block_col, inv_blocks):
    own_ids = jnp.arange(NCLUS, dtype=jnp.int32)[:, None]
    cluster_table = jnp.concatenate([own_ids, margin_ids.astype(jnp.int32)], axis=1)

    def one_subdomain(items):
        cluster_ids, rows_here, cols_here, blocks_here = items
        gathered = residual[cluster_ids].astype(jnp.float32)
        picked = gathered[cols_here]
        weights = blocks_here.astype(jnp.float32)
        products = jnp.einsum("bmap,bnpq->bmnaq", picked, weights)
        real_part = products[:, 0, 0] - products[:, 1, 1]
        imag_part = products[:, 0, 1] + products[:, 1, 0]
        block_out = jnp.stack([real_part, imag_part], axis=1)
        summed = jax.ops.segment_sum(block_out, rows_here, num_segments=K)
        return summed.astype(jnp.bfloat16)

    slot_out = lax.map(one_subdomain, (cluster_table, block_row, block_col, inv_blocks))
    flat_out = slot_out.reshape(NCLUS * K, 2, ANGLES, P_SIZE).astype(jnp.float32)
    return jax.ops.segment_sum(flat_out, cluster_table.reshape(-1), num_segments=NCLUS)
```

```python
import functools

import jax
import jax.numpy as jnp
from jax import lax
from jax.experimental import pallas as pl
from jax.experimental.pallas import tpu as pltpu
from jax.sharding import PartitionSpec as P

MESH = pl.DeviceIdType.MESH


def apply_blocks(sub_rows, block_sub, block_rows, block_cols, block_vals):
    sub_count, slot_count, halves, angle_count, panels = sub_rows.shape
    block_count = block_vals.shape[0]
    flat_inputs = sub_rows.reshape(sub_count * slot_count, halves * angle_count * panels)
    positions = jnp.arange(sub_count * slot_count, dtype=jnp.int32)
    col_index = block_sub * slot_count + block_cols
    col_pick = (col_index[:, None] == positions[None, :]).astype(jnp.bfloat16)
    block_input = jnp.dot(col_pick, flat_inputs, preferred_element_type=jnp.float32).astype(
        jnp.bfloat16
    )
    block_input = block_input.reshape(block_count, halves, angle_count, panels)
    products = jnp.einsum(
        "bmap,bnpq->bmnaq", block_input, block_vals, preferred_element_type=jnp.float32
    )
    real_part = products[:, 0, 0] - products[:, 1, 1]
    imag_part = products[:, 0, 1] + products[:, 1, 0]
    block_out = jnp.stack([real_part, imag_part], axis=1).reshape(
        block_count, halves * angle_count * panels
    )
    row_index = block_sub * slot_count + block_rows
    row_pick = (positions[:, None] == row_index[None, :]).astype(jnp.float32)
    summed = jnp.dot(
        row_pick, block_out, precision=lax.Precision.HIGHEST, preferred_element_type=jnp.float32
    )
    return summed.reshape(sub_count * slot_count, halves, angle_count, panels)


def shards(residual, margin_ids, block_row, block_col, inv_blocks):
    peer_count = lax.axis_size("clus")
    my_index = lax.axis_index("clus")
    clusters, halves, angle_count, panels = residual.shape
    remote = margin_ids.shape[1]
    slot_count = remote + 1
    blocks_each = block_row.shape[1]
    request_count = clusters * remote
    capacity = (request_count + peer_count - 2) // (peer_count - 1)
    feature_count = halves * angle_count * panels
    requests = margin_ids.reshape(peer_count, request_count)
    owners = requests // clusters
    local_ids = requests % clusters
    to_me = (owners == my_index).astype(jnp.int32)
    ranking = jnp.cumsum(to_me, axis=1) - 1
    slot_range = jnp.arange(capacity, dtype=jnp.int32)
    matched = (to_me[:, :, None] == 1) & (ranking[:, :, None] == slot_range[None, None, :])
    chosen = matched[:, :, :, None] & (
        local_ids[:, :, None, None] == jnp.arange(clusters, dtype=jnp.int32)
    )
    selector = jnp.any(chosen, axis=1).reshape(peer_count * capacity, clusters).astype(jnp.bfloat16)
    flat_rows = residual.reshape(clusters, feature_count)
    outgoing = jnp.dot(selector, flat_rows, preferred_element_type=jnp.float32).astype(jnp.bfloat16)
    outgoing = outgoing.reshape(peer_count, capacity, halves, angle_count, panels)
    incoming = lax.all_to_all(outgoing, "clus", split_axis=0, concat_axis=0, tiled=True)
    targets = lax.dynamic_index_in_dim(owners, my_index, 0, keepdims=False)
    order_ids = jnp.arange(request_count, dtype=jnp.int32)
    earlier = (targets[:, None] == targets[None, :]) & (order_ids[:, None] > order_ids[None, :])
    my_ranks = jnp.sum(earlier.astype(jnp.int32), axis=1)
    slot_index = targets * capacity + my_ranks
    remote_rows = incoming.reshape(peer_count * capacity, halves, angle_count, panels)[slot_index]
    remote_rows = remote_rows.reshape(clusters, remote, halves, angle_count, panels)
    sub_rows = jnp.concatenate([residual[:, None], remote_rows], axis=1)
    block_sub = jnp.broadcast_to(
        jnp.arange(clusters, dtype=jnp.int32)[:, None], (clusters, blocks_each)
    ).reshape(-1)
    flat_block_rows = block_row.reshape(-1)
    flat_block_cols = block_col.reshape(-1)
    block_vals = inv_blocks.reshape(clusters * blocks_each, halves, panels, panels)
    slot_sums = apply_blocks(sub_rows, block_sub, flat_block_rows, flat_block_cols, block_vals)
    rounded = slot_sums.astype(jnp.bfloat16).reshape(clusters, slot_count, feature_count)
    own_part = rounded[:, 0]
    remote_part = rounded[:, 1:].reshape(request_count, feature_count)
    slot_ids = jnp.arange(peer_count * capacity, dtype=jnp.int32)
    placer = (slot_ids[:, None] == slot_index[None, :]).astype(jnp.bfloat16)
    returning = jnp.dot(placer, remote_part, preferred_element_type=jnp.float32).astype(
        jnp.bfloat16
    )
    returning = returning.reshape(peer_count, capacity, halves, angle_count, panels)
    returned = lax.all_to_all(returning, "clus", split_axis=0, concat_axis=0, tiled=True)
    gathered_sums = jnp.einsum(
        "rc,rf->cf",
        selector,
        returned.reshape(peer_count * capacity, feature_count),
        preferred_element_type=jnp.float32,
    )
    combined = own_part.astype(jnp.float32) + gathered_sums
    return combined.reshape(clusters, halves, angle_count, panels)

def UP(n):
    return range(n)


def RORDER(me, n):
    return [lax.rem(me + d, n) for d in range(1, n)]


def fused_kernel(
    n,
    ids_hbm,
    rows_hbm,
    cols_hbm,
    res_hbm,
    inv_ref,
    out_ref,
    ids_ref,
    rows_ref,
    cols_ref,
    gathered,
    weights,
    block_out,
    place_t,
    send_buf,
    recv_buf,
    in_sem,
    w_sem,
    ready,
    gs_sem,
    gr_sem,
    ss_sem,
    sr_sem,
):
    me = lax.axis_index("clus")
    clusters, part, panels = res_hbm.shape
    angles = part // 2
    blocks = rows_ref.shape[1]
    kp = place_t.shape[0]
    total = clusters * blocks
    barrier = pltpu.get_barrier_semaphore()

    def at(peer):
        return {"clus": peer}

    for e in range(1, n):

        @pl.when(e > me)
        def _():
            pl.semaphore_signal(barrier, inc=1, device_id=at(e), device_id_type=MESH)

    mine = gathered.at[pl.ds(me * clusters, clusters)]
    own_copy = pltpu.make_async_copy(res_hbm, mine, in_sem.at[0])
    own_copy.start()
    tables = [
        pltpu.make_async_copy(source, table, in_sem.at[1 + i])
        for i, (source, table) in enumerate(
            ((ids_hbm, ids_ref), (rows_hbm, rows_ref), (cols_hbm, cols_ref))
        )
    ]
    for copy in tables:
        copy.start()

    @pl.when(me > 0)
    def _():
        pl.semaphore_wait(barrier, me)

    for e in range(n - 1):

        @pl.when(e < me)
        def _():
            pl.semaphore_signal(ready.at[me], inc=1, device_id=at(e), device_id_type=MESH)

    w_copies = [
        pltpu.make_async_copy(inv_ref.at[s], weights.at[s], w_sem.at[s]) for s in range(clusters)
    ]
    for copy in w_copies:
        copy.start()

    def gather(peer, source):
        rows = gathered.at[pl.ds(source * clusters, clusters)]
        return pltpu.make_async_remote_copy(
            src_ref=rows,
            dst_ref=rows,
            send_sem=gs_sem.at[peer],
            recv_sem=gr_sem.at[source],
            device_id=at(peer),
            device_id_type=MESH,
        )

    def send_back(peer, source):
        return pltpu.make_async_remote_copy(
            src_ref=send_buf.at[peer],
            dst_ref=recv_buf.at[source],
            send_sem=ss_sem.at[peer],
            recv_sem=sr_sem.at[source],
            device_id=at(peer),
            device_id_type=MESH,
        )

    own_copy.wait()
    for e in UP(n):

        @pl.when(e < me)
        def _():
            gather(e, me).start()

    block_out[pl.ds(total * part, (kp - total) * part), :] = jnp.zeros(
        ((kp - total) * part, panels), jnp.float32
    )
    place_t[...] = jnp.zeros_like(place_t)
    lanes = lax.broadcasted_iota(jnp.int32, (1, place_t.shape[1]), 1)

    for copy in tables:
        copy.wait()

    def place_rows(s, carry):
        sub = me * clusters + s
        for b in range(blocks):
            slot = rows_ref[s, b]
            margin = ids_ref[jnp.maximum(slot - 1, 0), sub]
            target = jnp.where(slot == 0, sub, margin)
            place_t[pl.ds(s * blocks + b, 1), :] = (lanes == target).astype(jnp.float32)
        return carry

    def send_down():
        for e in range(1, n):

            @pl.when(e > me)
            def _():
                pl.semaphore_wait(ready.at[e], 1)
                gather(e, me).start()

    lax.fori_loop(0, clusters, place_rows, 0)
    place = jnp.transpose(place_t[...])[: n * clusters].astype(jnp.bfloat16)
    send_down()

    for copy in w_copies:
        copy.wait()
    for d in range(1, n):
        source = lax.rem(me + d, n)
        gather(source, source).wait_recv()

    def subdomain(s, carry):
        sub = me * clusters + s
        for b in range(blocks):
            slot = cols_ref[s, b]
            margin = ids_ref[jnp.maximum(slot - 1, 0), sub]
            source = jnp.where(slot == 0, sub, margin)
            x = gathered[source]
            both = jnp.concatenate([weights[s, b, 0], weights[s, b, 1]], axis=1)
            both = jnp.dot(x, both, preferred_element_type=jnp.float32)
            real, imag = both[:, :panels], both[:, panels:]
            start = pl.multiple_of((s * blocks + b) * part, part)
            block_out[pl.ds(start, angles), :] = real[:angles] - imag[angles:]
            block_out[pl.ds(start + angles, angles), :] = imag[:angles] + real[angles:]
        return carry

    lax.fori_loop(0, clusters, subdomain, 0, unroll=4)

    for a in range(part):
        picked = block_out[pl.ds(a, kp, stride=part), :].astype(jnp.bfloat16)
        sums = jnp.dot(place, picked, preferred_element_type=jnp.float32)
        send_buf[:, a] = sums.reshape(n, clusters, panels).astype(jnp.bfloat16)

    for peer in RORDER(me, n):
        if isinstance(peer, tuple):
            peer, cond = peer

            @pl.when(cond)
            def _():
                send_back(peer, me).start()
        else:
            send_back(peer, me).start()

    acc = [send_buf[me, a].astype(jnp.float32) for a in range(part)]
    for d in range(1, n):
        source = lax.rem(me + d, n)
        send_back(source, source).wait_recv()
        acc = [acc[a] + recv_buf[source, a].astype(jnp.float32) for a in range(part)]
    for a in range(part):
        out_ref[pl.ds(a, clusters, stride=part), :] = acc[a]
    for d in range(1, n):
        peer = lax.rem(me + d, n)
        gather(peer, me).wait_send()
        send_back(peer, me).wait_send()


def fused(n, residual, margin_ids, block_row, block_col, inv_blocks):
    clusters, halves, angle_count, panels = residual.shape
    blocks = block_row.shape[1]
    part = halves * angle_count
    kp = -(-clusters * blocks // 128) * 128
    mp = -(-clusters * n // 128) * 128
    hbm = pl.BlockSpec(memory_space=pl.ANY)
    vmem = pl.BlockSpec(memory_space=pltpu.VMEM)
    out = pl.pallas_call(
        functools.partial(fused_kernel, n),
        out_shape=pltpu.VMEM((clusters * part, panels), jnp.float32),
        in_specs=[hbm] * 5,
        out_specs=vmem,
        scratch_shapes=[
            pltpu.SMEM(margin_ids.shape[::-1], jnp.int32),
            pltpu.SMEM(block_row.shape, jnp.int32),
            pltpu.SMEM(block_col.shape, jnp.int32),
            pltpu.VMEM((n * clusters, part, panels), jnp.bfloat16),
            pltpu.VMEM(inv_blocks.shape, jnp.bfloat16),
            pltpu.VMEM((kp * part, panels), jnp.float32),
            pltpu.VMEM((kp, mp), jnp.float32),
            pltpu.VMEM((n, part, clusters, panels), jnp.bfloat16),
            pltpu.VMEM((n, part, clusters, panels), jnp.bfloat16),
            pltpu.SemaphoreType.DMA((4,)),
            pltpu.SemaphoreType.DMA((clusters,)),
            pltpu.SemaphoreType.REGULAR((n,)),
            pltpu.SemaphoreType.DMA((n,)),
            pltpu.SemaphoreType.DMA((n,)),
            pltpu.SemaphoreType.DMA((n,)),
            pltpu.SemaphoreType.DMA((n,)),
        ],
        compiler_params=pltpu.CompilerParams(collective_id=0, has_side_effects=True),
    )(
        margin_ids.T,
        block_row,
        block_col,
        residual.reshape(clusters, part, panels),
        inv_blocks,
    )
    return out.reshape(clusters, halves, angle_count, panels)


def apply_device(residual, margin_ids, block_row, block_col, inv_blocks):
    n = lax.axis_size("clus")
    clusters = residual.shape[0]
    capacity = (clusters * margin_ids.shape[1] + n - 2) // (n - 1)
    body = functools.partial(fused, n) if capacity >= clusters else shards
    return body(residual, margin_ids, block_row, block_col, inv_blocks)


def solution(mesh):
    return jax.shard_map(
        apply_device,
        mesh=mesh,
        in_specs=(
            P("clus", None, "ang", None),
            P(),
            P("clus", None),
            P("clus", None),
            P("clus", None, None, None, None),
        ),
        out_specs=P("clus", None, "ang", None),
        check_vma=False,
    )
```

```python
import functools

import jax
import jax.numpy as jnp
from jax import lax
from jax.experimental import pallas as pl
from jax.experimental.pallas import tpu as pltpu
from jax.sharding import PartitionSpec as P

MESH = pl.DeviceIdType.MESH
GATHER_MASKS = (7, 2, 5, 6, 3, 4, 1)


def apply_blocks(sub_rows, block_sub, block_rows, block_cols, block_vals):
    sub_count, slot_count, halves, angle_count, panels = sub_rows.shape
    block_count = block_vals.shape[0]
    flat_inputs = sub_rows.reshape(sub_count * slot_count, halves * angle_count * panels)
    positions = jnp.arange(sub_count * slot_count, dtype=jnp.int32)
    col_index = block_sub * slot_count + block_cols
    col_pick = (col_index[:, None] == positions[None, :]).astype(jnp.bfloat16)
    block_input = jnp.dot(col_pick, flat_inputs, preferred_element_type=jnp.float32).astype(
        jnp.bfloat16
    )
    block_input = block_input.reshape(block_count, halves, angle_count, panels)
    products = jnp.einsum(
        "bmap,bnpq->bmnaq", block_input, block_vals, preferred_element_type=jnp.float32
    )
    real_part = products[:, 0, 0] - products[:, 1, 1]
    imag_part = products[:, 0, 1] + products[:, 1, 0]
    block_out = jnp.stack([real_part, imag_part], axis=1).reshape(
        block_count, halves * angle_count * panels
    )
    row_index = block_sub * slot_count + block_rows
    row_pick = (positions[:, None] == row_index[None, :]).astype(jnp.float32)
    summed = jnp.dot(
        row_pick, block_out, precision=lax.Precision.HIGHEST, preferred_element_type=jnp.float32
    )
    return summed.reshape(sub_count * slot_count, halves, angle_count, panels)


def shards(residual, margin_ids, block_row, block_col, inv_blocks):
    peer_count = lax.axis_size("clus")
    my_index = lax.axis_index("clus")
    clusters, halves, angle_count, panels = residual.shape
    remote = margin_ids.shape[1]
    slot_count = remote + 1
    blocks_each = block_row.shape[1]
    request_count = clusters * remote
    capacity = (request_count + peer_count - 2) // (peer_count - 1)
    feature_count = halves * angle_count * panels
    requests = margin_ids.reshape(peer_count, request_count)
    owners = requests // clusters
    local_ids = requests % clusters
    to_me = (owners == my_index).astype(jnp.int32)
    ranking = jnp.cumsum(to_me, axis=1) - 1
    slot_range = jnp.arange(capacity, dtype=jnp.int32)
    matched = (to_me[:, :, None] == 1) & (ranking[:, :, None] == slot_range[None, None, :])
    chosen = matched[:, :, :, None] & (
        local_ids[:, :, None, None] == jnp.arange(clusters, dtype=jnp.int32)
    )
    selector = jnp.any(chosen, axis=1).reshape(peer_count * capacity, clusters).astype(jnp.bfloat16)
    flat_rows = residual.reshape(clusters, feature_count)
    outgoing = jnp.dot(selector, flat_rows, preferred_element_type=jnp.float32).astype(jnp.bfloat16)
    outgoing = outgoing.reshape(peer_count, capacity, halves, angle_count, panels)
    incoming = lax.all_to_all(outgoing, "clus", split_axis=0, concat_axis=0, tiled=True)
    targets = lax.dynamic_index_in_dim(owners, my_index, 0, keepdims=False)
    order_ids = jnp.arange(request_count, dtype=jnp.int32)
    earlier = (targets[:, None] == targets[None, :]) & (order_ids[:, None] > order_ids[None, :])
    my_ranks = jnp.sum(earlier.astype(jnp.int32), axis=1)
    slot_index = targets * capacity + my_ranks
    remote_rows = incoming.reshape(peer_count * capacity, halves, angle_count, panels)[slot_index]
    remote_rows = remote_rows.reshape(clusters, remote, halves, angle_count, panels)
    sub_rows = jnp.concatenate([residual[:, None], remote_rows], axis=1)
    block_sub = jnp.broadcast_to(
        jnp.arange(clusters, dtype=jnp.int32)[:, None], (clusters, blocks_each)
    ).reshape(-1)
    flat_block_rows = block_row.reshape(-1)
    flat_block_cols = block_col.reshape(-1)
    block_vals = inv_blocks.reshape(clusters * blocks_each, halves, panels, panels)
    slot_sums = apply_blocks(sub_rows, block_sub, flat_block_rows, flat_block_cols, block_vals)
    rounded = slot_sums.astype(jnp.bfloat16).reshape(clusters, slot_count, feature_count)
    own_part = rounded[:, 0]
    remote_part = rounded[:, 1:].reshape(request_count, feature_count)
    slot_ids = jnp.arange(peer_count * capacity, dtype=jnp.int32)
    placer = (slot_ids[:, None] == slot_index[None, :]).astype(jnp.bfloat16)
    returning = jnp.dot(placer, remote_part, preferred_element_type=jnp.float32).astype(
        jnp.bfloat16
    )
    returning = returning.reshape(peer_count, capacity, halves, angle_count, panels)
    returned = lax.all_to_all(returning, "clus", split_axis=0, concat_axis=0, tiled=True)
    gathered_sums = jnp.einsum(
        "rc,rf->cf",
        selector,
        returned.reshape(peer_count * capacity, feature_count),
        preferred_element_type=jnp.float32,
    )
    combined = own_part.astype(jnp.float32) + gathered_sums
    return combined.reshape(clusters, halves, angle_count, panels)

def gather_order(me, n):
    if n == len(GATHER_MASKS) + 1:
        return [lax.bitwise_xor(me, jnp.int32(mask)) for mask in GATHER_MASKS]
    return [lax.rem(me + d, n) for d in range(1, n)]


def fused_kernel(
    n,
    ids_hbm,
    rows_hbm,
    cols_hbm,
    res_hbm,
    inv_ref,
    out_ref,
    ids_ref,
    rows_ref,
    cols_ref,
    gathered,
    weights,
    block_out,
    place_t,
    send_buf,
    recv_buf,
    in_sem,
    w_sem,
    gs_sem,
    gr_sem,
    ss_sem,
    sr_sem,
):
    me = lax.axis_index("clus")
    clusters, part, panels = res_hbm.shape
    angles = part // 2
    blocks = rows_ref.shape[1]
    kp = place_t.shape[0]
    total = clusters * blocks
    barrier = pltpu.get_barrier_semaphore()

    def at(peer):
        return {"clus": peer}

    for d in range(1, n):
        pl.semaphore_signal(barrier, inc=1, device_id=at(lax.rem(me + d, n)), device_id_type=MESH)

    mine = gathered.at[pl.ds(me * clusters, clusters)]
    own_copy = pltpu.make_async_copy(res_hbm, mine, in_sem.at[0])
    own_copy.start()
    tables = [
        pltpu.make_async_copy(source, table, in_sem.at[1 + i])
        for i, (source, table) in enumerate(
            ((ids_hbm, ids_ref), (rows_hbm, rows_ref), (cols_hbm, cols_ref))
        )
    ]
    for copy in tables:
        copy.start()

    w_copies = [
        pltpu.make_async_copy(inv_ref.at[s], weights.at[s], w_sem.at[s]) for s in range(clusters)
    ]
    for copy in w_copies:
        copy.start()

    def gather(peer, source):
        rows = gathered.at[pl.ds(source * clusters, clusters)]
        return pltpu.make_async_remote_copy(
            src_ref=rows,
            dst_ref=rows,
            send_sem=gs_sem.at[peer],
            recv_sem=gr_sem.at[source],
            device_id=at(peer),
            device_id_type=MESH,
        )

    def send_back(peer, source):
        return pltpu.make_async_remote_copy(
            src_ref=send_buf.at[peer],
            dst_ref=recv_buf.at[source],
            send_sem=ss_sem.at[peer],
            recv_sem=sr_sem.at[source],
            device_id=at(peer),
            device_id_type=MESH,
        )

    block_out[pl.ds(total * part, (kp - total) * part), :] = jnp.zeros(
        ((kp - total) * part, panels), jnp.float32
    )
    place_t[...] = jnp.zeros_like(place_t)
    lanes = lax.broadcasted_iota(jnp.int32, (1, place_t.shape[1]), 1)

    for copy in tables:
        copy.wait()

    def place_rows(s, carry):
        sub = me * clusters + s
        for b in range(blocks):
            slot = rows_ref[s, b]
            margin = ids_ref[jnp.maximum(slot - 1, 0), sub]
            target = jnp.where(slot == 0, sub, margin)
            place_t[pl.ds(s * blocks + b, 1), :] = (lanes == target).astype(jnp.float32)
        return carry

    lax.fori_loop(0, clusters, place_rows, 0)
    place = jnp.transpose(place_t[...])[: n * clusters].astype(jnp.bfloat16)
    own_copy.wait()
    pl.semaphore_wait(barrier, n - 1)
    for peer in gather_order(me, n):
        gather(peer, me).start()

    for copy in w_copies:
        copy.wait()
    for d in range(1, n):
        source = lax.rem(me + d, n)
        gather(source, source).wait_recv()

    def subdomain(s, carry):
        sub = me * clusters + s
        for b in range(blocks):
            slot = cols_ref[s, b]
            margin = ids_ref[jnp.maximum(slot - 1, 0), sub]
            source = jnp.where(slot == 0, sub, margin)
            x = gathered[source]
            turned = jnp.concatenate([-x[angles:], x[:angles]], axis=0)
            both = jnp.concatenate([x, turned], axis=1)
            start = pl.multiple_of((s * blocks + b) * part, part)
            block_out[pl.ds(start, part), :] = jnp.dot(
                both, weights[s, b], preferred_element_type=jnp.float32
            )
        return carry

    lax.fori_loop(0, clusters, subdomain, 0, unroll=4)

    for a in range(part):
        picked = block_out[pl.ds(a, kp, stride=part), :].astype(jnp.bfloat16)
        sums = jnp.dot(place, picked, preferred_element_type=jnp.float32)
        send_buf[:, a] = sums.reshape(n, clusters, panels).astype(jnp.bfloat16)

    for d in range(1, n):
        send_back(lax.rem(me + d, n), me).start()

    for d in range(1, n):
        gather(lax.rem(me + d, n), me).wait_send()
    acc = [send_buf[me, a].astype(jnp.float32) for a in range(part)]
    for d in range(1, n):
        if d == n - 1:
            for k in range(1, n):
                send_back(lax.rem(me + k, n), me).wait_send()
        source = lax.rem(me + d, n)
        send_back(source, source).wait_recv()
        acc = [acc[a] + recv_buf[source, a].astype(jnp.float32) for a in range(part)]
    for a in range(part):
        out_ref[pl.ds(a, clusters, stride=part), :] = acc[a]


def fused(n, residual, margin_ids, block_row, block_col, inv_blocks):
    clusters, halves, angle_count, panels = residual.shape
    blocks = block_row.shape[1]
    part = halves * angle_count
    kp = -(-clusters * blocks // 128) * 128
    mp = -(-clusters * n // 128) * 128
    hbm = pl.BlockSpec(memory_space=pl.ANY)
    vmem = pl.BlockSpec(memory_space=pltpu.VMEM)
    out = pl.pallas_call(
        functools.partial(fused_kernel, n),
        out_shape=pltpu.VMEM((clusters * part, panels), jnp.float32),
        in_specs=[hbm] * 5,
        out_specs=vmem,
        scratch_shapes=[
            pltpu.SMEM(margin_ids.shape[::-1], jnp.int32),
            pltpu.SMEM(block_row.shape, jnp.int32),
            pltpu.SMEM(block_col.shape, jnp.int32),
            pltpu.VMEM((n * clusters, part, panels), jnp.bfloat16),
            pltpu.VMEM((clusters, blocks, 2 * panels, panels), jnp.bfloat16),
            pltpu.VMEM((kp * part, panels), jnp.float32),
            pltpu.VMEM((kp, mp), jnp.float32),
            pltpu.VMEM((n, part, clusters, panels), jnp.bfloat16),
            pltpu.VMEM((n, part, clusters, panels), jnp.bfloat16),
            pltpu.SemaphoreType.DMA((4,)),
            pltpu.SemaphoreType.DMA((clusters,)),
            pltpu.SemaphoreType.DMA((n,)),
            pltpu.SemaphoreType.DMA((n,)),
            pltpu.SemaphoreType.DMA((n,)),
            pltpu.SemaphoreType.DMA((n,)),
        ],
        compiler_params=pltpu.CompilerParams(collective_id=0, has_side_effects=True),
    )(
        margin_ids.T,
        block_row,
        block_col,
        residual.reshape(clusters, part, panels),
        inv_blocks.reshape(clusters, blocks, 2 * panels, panels),
    )
    return out.reshape(clusters, halves, angle_count, panels)


def apply_device(residual, margin_ids, block_row, block_col, inv_blocks):
    n = lax.axis_size("clus")
    clusters = residual.shape[0]
    capacity = (clusters * margin_ids.shape[1] + n - 2) // (n - 1)
    body = functools.partial(fused, n) if capacity >= clusters else shards
    return body(residual, margin_ids, block_row, block_col, inv_blocks)


def solution(mesh):
    return jax.shard_map(
        apply_device,
        mesh=mesh,
        in_specs=(
            P("clus", None, "ang", None),
            P(),
            P("clus", None),
            P("clus", None),
            P("clus", None, None, None, None),
        ),
        out_specs=P("clus", None, "ang", None),
        check_vma=False,
    )
```
